256 devices in a mesh: wide: 32 (over z_hi, y, x), narrow: 8 (over z_lo, core).
Axes of the slice: x: 4, y: 4, z: 8 (z_hi: 2, z_lo: 4; z = z_hi * 4 + z_lo), core: 2. Of those that a mesh axis runs over, the one named last changes fastest.
Arguments:
- tile_pool: bfloat16 [32, 1024, 768], P('wide', 'narrow'), may hold values from -96 to 96
- batch_index: int32 [32, 2048], P('wide', 'narrow'), may hold values from 0 to 127
- pair_label: int32 [32, 2048], P('wide', 'narrow'), may hold values from 0 to 255, as said below
- w_first: bfloat16 [768, 2048], P('narrow'), may hold values from -0.375 to 0.375
- w_second: bfloat16 [2048, 2048], P('narrow'), may hold values from -0.375 to 0.375
- m_first: bfloat16 [32, 768, 2048], P('wide', 'narrow'), may hold values from -0.01275776 to 0.01275776
- m_second: bfloat16 [32, 2048, 2048], P('wide', 'narrow'), may hold values from -0.0078125 to 0.0078125
- v_first: bfloat16 [32, 768, 2048], P('wide', 'narrow'), may hold values from 0.0005086263 to 0.025431315
- v_second: bfloat16 [32, 2048, 2048], P('wide', 'narrow'), may hold values from 0.00019073486 to 0.009536743
- mom_first: bfloat16 [768, 2048], P('narrow'), may hold values from -0.1796875 to 0.1796875
- mom_second: bfloat16 [2048, 2048], P('narrow'), may hold values from -0.1796875 to 0.1796875
Outputs:
- new_first: bfloat16 [768, 2048], P('narrow')
- new_second: bfloat16 [2048, 2048], P('narrow')
- mom_out_first: bfloat16 [768, 2048], P('narrow')
- mom_out_second: bfloat16 [2048, 2048], P('narrow')
The draws below stay inside these ranges and needn't reach their ends.
Inputs may be any that keep to these rules, and one draw needn't show every extreme that they name: `batch_index`: indices count within the pool of the same site and shard. `pair_label`: each row's partner is another row of the same site and shard, counted within that shard's 256 rows, and names the row back.
All inputs are finite; a program needn't handle non-finite values.
Results may differ from the reference program's by a relative error of at most 0.0075.
Values may be sent and summed in bfloat16 or wider, within the bound.
A program may use at most 128 MiB of HBM per device.

```python
import math
import jax
import jax.numpy as jnp
from jax import lax

PIX = 768
MID = 2048
OUT = 2048
ROWS_DEV = 256
POOL_DEV = 128
SITES = 32
SHARDS = 8


def draw_pair_label(key, part):
    blocks = SITES * SHARDS
    block_keys = jax.random.split(jax.random.fold_in(key, 7), blocks)

    def one_block(block_key):
        order = jax.random.permutation(block_key, ROWS_DEV).astype(jnp.int32)
        couples = order.reshape(ROWS_DEV // 2, 2)
        partner = couples[:, ::-1].reshape(ROWS_DEV)
        return jnp.zeros((ROWS_DEV,), jnp.int32).at[order].set(partner)
    return jax.vmap(one_block)(block_keys).reshape(SITES, SHARDS * ROWS_DEV)


def first_spread():
    return 400.0 * math.sqrt(SHARDS * ROWS_DEV / (OUT * MID * PIX))


def second_spread():
    return 400.0 / OUT


def moment_values(moment_key, array_shape, spread):
    deviation = 0.01 * spread
    normal_draw = jax.random.normal(moment_key, array_shape, jnp.float32)
    sampled = jnp.clip(normal_draw, -3.96, 3.96) * deviation
    return sampled.astype(jnp.bfloat16)


def square_values(moment_key, array_shape, spread):
    lowest = 0.005 * spread * spread
    uniform_draw = jax.random.uniform(moment_key, array_shape, jnp.float32)
    levels = 0.002 + 0.996 * uniform_draw
    sampled = lowest * jnp.exp(math.log(50.0) * levels)
    return sampled.astype(jnp.bfloat16)


def draw_m_first(key, part):
    return moment_values(jax.random.fold_in(key, 11), (SITES, PIX, MID), first_spread())


def draw_m_second(key, part):
    return moment_values(jax.random.fold_in(key, 13), (SITES, MID, OUT), second_spread())


def draw_v_first(key, part):
    return square_values(jax.random.fold_in(key, 17), (SITES, PIX, MID), first_spread())


def draw_v_second(key, part):
    return square_values(jax.random.fold_in(key, 19), (SITES, MID, OUT), second_spread())


def touch_ends(values, stream_key, smallest, largest):
    dims = values.shape
    spot = [jax.random.randint(jax.random.fold_in(stream_key, axis), (), 0, dims[axis]) for axis in range(len(dims))]
    values = values.at[tuple(spot)].set(smallest)
    longest = dims.index(max(dims))
    spot[longest] = (spot[longest] + 1) % dims[longest]
    return values.at[tuple(spot)].set(largest)


def block_levels(stream_key, dims, cuts, smallest, largest):
    loudness, own = 1.0, jax.random.fold_in(stream_key, 6)
    for dim, blocks in cuts:
        draws = jnp.exp(jax.random.uniform(jax.random.fold_in(own, dim), (blocks,), jnp.float32, smallest / len(cuts), largest / len(cuts)))
        loudness = loudness * jnp.repeat(draws, dims[dim] // blocks).reshape([-1 if axis == dim else 1 for axis in range(len(dims))])
    return loudness


def noise(stream_key, shape, scale, bound, cuts=(), kind=jnp.bfloat16):
    drawn = scale * jax.random.normal(stream_key, shape, jnp.float32)
    if cuts:
        drawn = drawn * block_levels(stream_key, shape, cuts, -0.22, 0.18)
    return jnp.clip(drawn, -bound, bound).astype(kind)


def setup_inputs(seed: int = 0) -> dict:
    splits = jax.random.split(jax.random.key(seed), 12)
    return {
        "tile_pool": noise(splits[0], (SITES, SHARDS * POOL_DEV, PIX), 16.0, 96.0, ((0, 32), (1, 8))),
        "batch_index": touch_ends(jax.random.randint(splits[1], (SITES, SHARDS * ROWS_DEV), 0, POOL_DEV), jax.random.fold_in(splits[1], 1), 0, POOL_DEV - 1).astype(jnp.int32),
        "pair_label": draw_pair_label(jax.random.fold_in(splits[11], 71), 0),
        "w_first": noise(splits[3], (PIX, MID), 0.0625, 0.375, ((0, 8),)),
        "w_second": noise(splits[4], (MID, OUT), 0.0625, 0.375, ((0, 8),)),
        "m_first": draw_m_first(jax.random.fold_in(splits[11], 71), 0),
        "m_second": draw_m_second(jax.random.fold_in(splits[11], 71), 0),
        "v_first": draw_v_first(jax.random.fold_in(splits[11], 71), 0),
        "v_second": draw_v_second(jax.random.fold_in(splits[11], 71), 0),
        "mom_first": noise(splits[9], (PIX, MID), 0.03, 0.1796875, ((0, 8),)),
        "mom_second": noise(splits[10], (MID, OUT), 0.03, 0.1796875, ((0, 8),)),
    }


logit_scale = 1.0 / 0.07
rate_inner = 0.2
weight_decay = 0.1
beta_first = 0.9
beta_second = 0.95
adam_eps = 1e-08
rate_outer = 0.7
momentum_coef = 0.9

def rounded(values):
    halves = lax.optimization_barrier(values.astype(jnp.bfloat16))
    return halves.astype(jnp.float32)

def device_terms(inputs, w_first, w_second, partner):
    scale_one = 1.0 / math.sqrt(PIX)
    scale_two = 1.0 / math.sqrt(MID)
    hidden = jnp.dot(inputs, w_first, preferred_element_type=jnp.float32) * scale_one
    active_full, gelu_back = jax.vjp(jax.nn.gelu, hidden)
    active = active_full.astype(jnp.bfloat16)
    embedded = jnp.dot(active, w_second, preferred_element_type=jnp.float32) * scale_two
    inverse = lax.rsqrt(lax.optimization_barrier(jnp.sum(embedded * embedded, axis=1, keepdims=True)) + OUT * 1e-06)
    unit_rows = embedded * inverse
    unit_half = unit_rows.astype(jnp.bfloat16)
    scores = logit_scale * jnp.dot(unit_half, unit_half.T, preferred_element_type=jnp.float32)
    positions = jnp.arange(inputs.shape[0], dtype=jnp.int32)
    diagonal = positions[:, None] == positions[None, :]
    scores = jnp.where(diagonal, -1e+30, scores)
    highest = lax.optimization_barrier(jnp.max(scores, axis=1, keepdims=True))
    powers = jnp.exp(scores - highest)
    softmax_rows = powers / lax.optimization_barrier(jnp.sum(powers, axis=1, keepdims=True))
    target = (partner[:, None] == positions[None, :]).astype(jnp.float32)
    score_grad = softmax_rows - target
    paired = (score_grad + score_grad.T).astype(jnp.bfloat16)
    unit_grad = logit_scale * jnp.dot(paired, unit_half, preferred_element_type=jnp.float32)
    embed_grad = inverse * (unit_grad - unit_rows * lax.optimization_barrier(jnp.sum(unit_rows * unit_grad, axis=1, keepdims=True)))
    embed_half = embed_grad.astype(jnp.bfloat16)
    term_second = scale_two * jnp.dot(active.T, embed_half, preferred_element_type=jnp.float32)
    active_grad = scale_two * jnp.dot(embed_half, w_second.T, preferred_element_type=jnp.float32)
    hidden_grad = gelu_back(active_grad)[0]
    hidden_half = hidden_grad.astype(jnp.bfloat16)
    term_first = scale_one * jnp.dot(inputs.T, hidden_half, preferred_element_type=jnp.float32)
    return (term_first, term_second)

def adam_delta(grads, first_moment, second_moment, weights):
    moment_one = beta_first * first_moment.astype(jnp.float32) + (1.0 - beta_first) * grads
    moment_two = beta_second * second_moment.astype(jnp.float32) + (1.0 - beta_second) * grads * grads
    return rate_inner * (moment_one / (jnp.sqrt(moment_two) + adam_eps) + weight_decay * weights.astype(jnp.float32))

def outer_update(delta, momentum, weights):
    velocity = momentum_coef * momentum.astype(jnp.float32) + delta
    updated = weights.astype(jnp.float32) - rate_outer * (delta + momentum_coef * velocity)
    return (updated.astype(jnp.bfloat16), velocity.astype(jnp.bfloat16))

def reference(tile_pool, batch_index, pair_label, w_first, w_second, m_first, m_second, v_first, v_second, mom_first, mom_second):
    pools = tile_pool.reshape(SITES, SHARDS, POOL_DEV, PIX)
    chosen = batch_index.reshape(SITES, SHARDS, ROWS_DEV)
    partners = pair_label.reshape(SITES, SHARDS, ROWS_DEV)
    zero_first = jnp.zeros((PIX, MID), jnp.float32)
    zero_second = jnp.zeros((MID, OUT), jnp.float32)

    def site_step(totals, items):
        site_pool, site_rows, site_partner, first_m, second_m, first_v, second_v = items

        def shard_step(sums, parts):
            shard_pool, shard_rows, shard_partner = parts
            inputs = jnp.take(shard_pool, shard_rows, axis=0)
            term_first, term_second = device_terms(inputs, w_first, w_second, shard_partner)
            return ((sums[0] + rounded(term_first), sums[1] + rounded(term_second)), None)
        grads, unused = lax.scan(shard_step, (zero_first, zero_second), (site_pool, site_rows, site_partner))
        delta_first = adam_delta(grads[0], first_m, first_v, w_first)
        delta_second = adam_delta(grads[1], second_m, second_v, w_second)
        return ((totals[0] + delta_first, totals[1] + delta_second), None)
    totals, unused = lax.scan(site_step, (zero_first, zero_second), (pools, chosen, partners, m_first, m_second, v_first, v_second))
    new_first, velocity_first = outer_update(totals[0] / SITES, mom_first, w_first)
    new_second, velocity_second = outer_update(totals[1] / SITES, mom_second, w_second)
    return (new_first, new_second, velocity_first, velocity_second)
```

```python
import math

import jax
import jax.numpy as jnp
import numpy as np
from jax import lax
from jax.sharding import Mesh
from jax.sharding import PartitionSpec as P

PIX = 768
MID = 2048
OUT = 2048


logit_scale = 1.0 / 0.07
rate_inner = 0.2
weight_decay = 0.1
beta_first = 0.9
beta_second = 0.95
adam_eps = 1e-08
rate_outer = 0.7
momentum_coef = 0.9

WIDE = ("zh", "y", "x")
NARROW = ("zl", "c")


def adam_delta(grads, first_moment, second_moment, weights):
    moment_one = beta_first * first_moment.astype(jnp.float32) + (1.0 - beta_first) * grads
    moment_two = (
        beta_second * second_moment.astype(jnp.float32) + (1.0 - beta_second) * grads * grads
    )
    return rate_inner * (
        moment_one / (jnp.sqrt(moment_two) + adam_eps) + weight_decay * weights.astype(jnp.float32)
    )


def outer_update(delta, momentum, weights):
    velocity = momentum_coef * momentum.astype(jnp.float32) + delta
    updated = weights.astype(jnp.float32) - rate_outer * (delta + momentum_coef * velocity)
    return (updated.astype(jnp.bfloat16), velocity.astype(jnp.bfloat16))


def embed_gradient(embedded, partner):
    inverse = lax.rsqrt(jnp.sum(embedded * embedded, axis=1, keepdims=True) + OUT * 1e-06)
    unit_rows = embedded * inverse
    unit_half = unit_rows.astype(jnp.bfloat16)
    scores = logit_scale * jnp.dot(unit_half, unit_half.T, preferred_element_type=jnp.float32)
    positions = jnp.arange(embedded.shape[0], dtype=jnp.int32)
    diagonal = positions[:, None] == positions[None, :]
    scores = jnp.where(diagonal, -1e30, scores)
    highest = jnp.max(scores, axis=1, keepdims=True)
    powers = jnp.exp(scores - highest)
    softmax_rows = powers / jnp.sum(powers, axis=1, keepdims=True)
    target = (partner[:, None] == positions[None, :]).astype(jnp.float32)
    score_grad = softmax_rows - target
    paired = (score_grad + score_grad.T).astype(jnp.bfloat16)
    unit_grad = logit_scale * jnp.dot(paired, unit_half, preferred_element_type=jnp.float32)
    embed_grad = inverse * (
        unit_grad - unit_rows * jnp.sum(unit_rows * unit_grad, axis=1, keepdims=True)
    )
    return embed_grad.astype(jnp.bfloat16)


def wide_mean_update(delta, momentum, weights):
    sites = lax.axis_size(WIDE)
    rows, cols = delta.shape
    piece = cols // sites
    got = lax.all_to_all(delta, WIDE, 1, 0, tiled=True)
    mean = jnp.sum(got.reshape(sites, rows, piece), axis=0) / sites
    start = lax.axis_index(WIDE) * piece
    mom_piece = lax.dynamic_slice_in_dim(momentum, start, piece, axis=1)
    w_piece = lax.dynamic_slice_in_dim(weights, start, piece, axis=1)
    new_piece, vel_piece = outer_update(mean, mom_piece, w_piece)
    both = jnp.concatenate([new_piece, vel_piece], axis=1)
    spread = jnp.broadcast_to(both[None], (sites,) + both.shape)
    back = lax.all_to_all(spread, WIDE, 0, 0, tiled=True)
    back = back.reshape(sites, rows, 2, piece).transpose(2, 1, 0, 3).reshape(2, rows, cols)
    return back[0], back[1]


def shards(
    tile_pool,
    batch_index,
    pair_label,
    w_first,
    w_second,
    m_first,
    m_second,
    v_first,
    v_second,
    mom_first,
    mom_second,
):
    inputs = jnp.take(tile_pool[0], batch_index[0], axis=0)
    partner = pair_label[0]
    scale_one = 1.0 / math.sqrt(PIX)
    scale_two = 1.0 / math.sqrt(MID)
    hidden = (
        jnp.dot(
            inputs,
            lax.all_gather(w_first, NARROW, axis=0, tiled=True),
            preferred_element_type=jnp.float32,
        )
        * scale_one
    )
    active_full, gelu_back = jax.vjp(jax.nn.gelu, hidden)
    active = active_full.astype(jnp.bfloat16)
    second_whole = lax.all_gather(w_second, NARROW, axis=0, tiled=True)
    embedded = jnp.dot(active, second_whole, preferred_element_type=jnp.float32) * scale_two
    embed_half = embed_gradient(embedded, partner)
    grad_second = lax.psum_scatter(
        (scale_two * jnp.dot(active.T, embed_half, preferred_element_type=jnp.float32)).astype(
            jnp.bfloat16
        ),
        NARROW,
        scatter_dimension=0,
        tiled=True,
    ).astype(jnp.float32)
    delta_second = adam_delta(grad_second, m_second[0], v_second[0], w_second)
    active_grad = scale_two * jnp.dot(
        embed_half, second_whole.T, preferred_element_type=jnp.float32
    )
    hidden_half = gelu_back(active_grad)[0].astype(jnp.bfloat16)
    grad_first = lax.psum_scatter(
        (scale_one * jnp.dot(inputs.T, hidden_half, preferred_element_type=jnp.float32)).astype(
            jnp.bfloat16
        ),
        NARROW,
        scatter_dimension=0,
        tiled=True,
    ).astype(jnp.float32)
    delta_first = adam_delta(grad_first, m_first[0], v_first[0], w_first)
    rows_first = delta_first.shape[0]
    new_w, vel = wide_mean_update(
        jnp.concatenate([delta_first, delta_second], axis=0),
        jnp.concatenate([mom_first, mom_second], axis=0),
        jnp.concatenate([w_first, w_second], axis=0),
    )
    return (new_w[:rows_first], new_w[rows_first:], vel[:rows_first], vel[rows_first:])


def solution(mesh):
    zh, y, x = 2, 4, 4
    devices = np.asarray(mesh.devices)
    wide, narrow = devices.shape
    sub = Mesh(devices.reshape(zh, y, x, narrow // 2, 2), WIDE + NARROW)
    site = P(WIDE, NARROW, None)
    rows = P(NARROW, None)
    return jax.shard_map(
        shards,
        mesh=sub,
        in_specs=(site, P(WIDE, NARROW), P(WIDE, NARROW), rows, rows, site, site, site, site, rows, rows),
        out_specs=(rows, rows, rows, rows),
        check_vma=False,
    )
```

```python
import math

import jax
import jax.numpy as jnp
import numpy as np
from jax import lax
from jax.sharding import Mesh
from jax.sharding import PartitionSpec as P

PIX = 768
MID = 2048
OUT = 2048


logit_scale = 1.0 / 0.07
rate_inner = 0.2
weight_decay = 0.1
beta_first = 0.9
beta_second = 0.95
adam_eps = 1e-08
rate_outer = 0.7
momentum_coef = 0.9

WIDE = ("zh", "y", "x")
NARROW = ("zl", "c")


def adam_delta(grads, first_moment, second_moment, weights):
    moment_one = beta_first * first_moment.astype(jnp.float32) + (1.0 - beta_first) * grads
    moment_two = (
        beta_second * second_moment.astype(jnp.float32) + (1.0 - beta_second) * grads * grads
    )
    return rate_inner * (
        moment_one / (jnp.sqrt(moment_two) + adam_eps) + weight_decay * weights.astype(jnp.float32)
    )


def outer_update(delta, momentum, weights):
    velocity = momentum_coef * momentum.astype(jnp.float32) + delta
    updated = weights.astype(jnp.float32) - rate_outer * (delta + momentum_coef * velocity)
    return (updated.astype(jnp.bfloat16), velocity.astype(jnp.bfloat16))


def embed_gradient(embedded, partner):
    inverse = lax.rsqrt(jnp.sum(embedded * embedded, axis=1, keepdims=True) + OUT * 1e-06)
    unit_rows = embedded * inverse
    unit_half = unit_rows.astype(jnp.bfloat16)
    scores = logit_scale * jnp.dot(unit_half, unit_half.T, preferred_element_type=jnp.float32)
    positions = jnp.arange(embedded.shape[0], dtype=jnp.int32)
    diagonal = positions[:, None] == positions[None, :]
    scores = jnp.where(diagonal, -1e30, scores)
    highest = jnp.max(scores, axis=1, keepdims=True)
    powers = jnp.exp(scores - highest)
    softmax_rows = powers / jnp.sum(powers, axis=1, keepdims=True)
    target = (partner[:, None] == positions[None, :]).astype(jnp.float32)
    score_grad = softmax_rows - target
    paired = (score_grad + score_grad.T).astype(jnp.bfloat16)
    unit_grad = logit_scale * jnp.dot(paired, unit_half, preferred_element_type=jnp.float32)
    embed_grad = inverse * (
        unit_grad - unit_rows * jnp.sum(unit_rows * unit_grad, axis=1, keepdims=True)
    )
    return embed_grad.astype(jnp.bfloat16)


def wide_mean_update(delta, momentum, weights, axis):
    sites = lax.axis_size(WIDE)
    piece = delta.shape[axis] // sites
    got = lax.all_to_all(delta, WIDE, axis, axis, tiled=True)
    got = jnp.moveaxis(got, axis, 0).reshape((sites, piece) + (delta.shape[1 - axis],))
    mean = jnp.moveaxis(jnp.sum(got, axis=0), 0, axis) / sites
    start = lax.axis_index(WIDE) * piece
    mom_piece = lax.dynamic_slice_in_dim(momentum, start, piece, axis=axis)
    w_piece = lax.dynamic_slice_in_dim(weights, start, piece, axis=axis)
    new_piece, vel_piece = outer_update(mean, mom_piece, w_piece)
    both = jnp.stack([new_piece, vel_piece], axis=0)
    spread = jnp.broadcast_to(both[None], (sites,) + both.shape)
    back = lax.all_to_all(spread, WIDE, 0, 0, tiled=True)
    back = jnp.moveaxis(back, 0, 1 + axis)
    shape = list(delta.shape)
    back = back.reshape([2] + shape)
    return back[0], back[1]


def shards(
    tile_pool,
    batch_index,
    pair_label,
    w_first,
    w_second,
    m_first,
    m_second,
    v_first,
    v_second,
    mom_first,
    mom_second,
):
    inputs = jnp.take(tile_pool[0], batch_index[0], axis=0)
    partner = pair_label[0]
    scale_one = 1.0 / math.sqrt(PIX)
    scale_two = 1.0 / math.sqrt(MID)
    hidden = (
        jnp.dot(
            inputs,
            lax.all_gather(w_first, NARROW, axis=0, tiled=True),
            preferred_element_type=jnp.float32,
        )
        * scale_one
    )
    active_full, gelu_back = jax.vjp(jax.nn.gelu, hidden)
    active = active_full.astype(jnp.bfloat16)
    second_whole = lax.all_gather(w_second, NARROW, axis=0, tiled=True)
    embedded = jnp.dot(active, second_whole, preferred_element_type=jnp.float32) * scale_two
    embed_half = embed_gradient(embedded, partner)
    active_grad = scale_two * jnp.dot(
        embed_half, second_whole.T, preferred_element_type=jnp.float32
    )
    hidden_half = gelu_back(active_grad)[0].astype(jnp.bfloat16)
    grad_first = lax.psum_scatter(
        (scale_one * jnp.dot(inputs.T, hidden_half, preferred_element_type=jnp.float32)).astype(
            jnp.bfloat16
        ),
        NARROW,
        scatter_dimension=0,
        tiled=True,
    ).astype(jnp.float32)
    delta_first = adam_delta(grad_first, m_first[0], v_first[0], w_first)
    new_first, vel_first = wide_mean_update(delta_first, mom_first, w_first, 1)
    term_second = (
        scale_two * jnp.dot(active.T, embed_half, preferred_element_type=jnp.float32)
    ).astype(jnp.bfloat16)
    halves = []
    cols = term_second.shape[1] // 2
    for h in range(2):
        part = slice(h * cols, (h + 1) * cols)
        grad_part = lax.psum_scatter(
            term_second[:, part], NARROW, scatter_dimension=0, tiled=True
        ).astype(jnp.float32)
        delta_part = adam_delta(
            grad_part, m_second[0][:, part], v_second[0][:, part], w_second[:, part]
        )
        halves.append(
            wide_mean_update(delta_part, mom_second[:, part], w_second[:, part], 0)
        )
    new_second = jnp.concatenate([halves[0][0], halves[1][0]], axis=1)
    vel_second = jnp.concatenate([halves[0][1], halves[1][1]], axis=1)
    return (new_first, new_second, vel_first, vel_second)


def solution(mesh):
    zh, y, x = 2, 4, 4
    devices = np.asarray(mesh.devices)
    wide, narrow = devices.shape
    sub = Mesh(devices.reshape(zh, y, x, narrow // 2, 2), WIDE + NARROW)
    site = P(WIDE, NARROW, None)
    rows = P(NARROW, None)
    return jax.shard_map(
        shards,
        mesh=sub,
        in_specs=(site, P(WIDE, NARROW), P(WIDE, NARROW), rows, rows, site, site, site, site, rows, rows),
        out_specs=(rows, rows, rows, rows),
        check_vma=False,
    )
```

```python
import math

import jax
import jax.numpy as jnp
import numpy as np
from jax import lax
from jax.sharding import Mesh
from jax.sharding import PartitionSpec as P

PIX = 768
MID = 2048
OUT = 2048


logit_scale = 1.0 / 0.07
rate_inner = 0.2
weight_decay = 0.1
beta_first = 0.9
beta_second = 0.95
adam_eps = 1e-08
rate_outer = 0.7
momentum_coef = 0.9

WIDE = ("zh", "y", "x")
NARROW = ("zl", "c")


def adam_delta(grads, first_moment, second_moment, weights):
    moment_one = beta_first * first_moment.astype(jnp.float32) + (1.0 - beta_first) * grads
    moment_two = (
        beta_second * second_moment.astype(jnp.float32) + (1.0 - beta_second) * grads * grads
    )
    return rate_inner * (
        moment_one / (jnp.sqrt(moment_two) + adam_eps) + weight_decay * weights.astype(jnp.float32)
    )


def outer_update(delta, momentum, weights):
    velocity = momentum_coef * momentum.astype(jnp.float32) + delta
    updated = weights.astype(jnp.float32) - rate_outer * (delta + momentum_coef * velocity)
    return (updated.astype(jnp.bfloat16), velocity.astype(jnp.bfloat16))


def embed_gradient(embedded, partner):
    inverse = lax.rsqrt(jnp.sum(embedded * embedded, axis=1, keepdims=True) + OUT * 1e-06)
    unit_rows = embedded * inverse
    unit_half = unit_rows.astype(jnp.bfloat16)
    scores = logit_scale * jnp.dot(unit_half, unit_half.T, preferred_element_type=jnp.float32)
    positions = jnp.arange(embedded.shape[0], dtype=jnp.int32)
    diagonal = positions[:, None] == positions[None, :]
    scores = jnp.where(diagonal, -1e30, scores)
    highest = jnp.max(scores, axis=1, keepdims=True)
    powers = jnp.exp(scores - highest)
    softmax_rows = powers / jnp.sum(powers, axis=1, keepdims=True)
    target = (partner[:, None] == positions[None, :]).astype(jnp.float32)
    score_grad = softmax_rows - target
    paired = (score_grad + score_grad.T).astype(jnp.bfloat16)
    unit_grad = logit_scale * jnp.dot(paired, unit_half, preferred_element_type=jnp.float32)
    embed_grad = inverse * (
        unit_grad - unit_rows * jnp.sum(unit_rows * unit_grad, axis=1, keepdims=True)
    )
    return embed_grad.astype(jnp.bfloat16)


def wide_mean_update(delta, momentum, weights):
    sites = lax.axis_size(WIDE)
    rows, cols = delta.shape
    piece = cols // sites
    got = lax.all_to_all(delta, WIDE, 1, 0, tiled=True)
    mean = jnp.sum(got.reshape(sites, rows, piece), axis=0) / sites
    start = lax.axis_index(WIDE) * piece
    mom_piece = lax.dynamic_slice_in_dim(momentum, start, piece, axis=1)
    w_piece = lax.dynamic_slice_in_dim(weights, start, piece, axis=1)
    new_piece, vel_piece = outer_update(mean, mom_piece, w_piece)
    both = jnp.concatenate([new_piece, vel_piece], axis=1)
    spread = jnp.broadcast_to(both[None], (sites,) + both.shape)
    back = lax.all_to_all(spread, WIDE, 0, 0, tiled=True)
    back = back.reshape(sites, rows, 2, piece).transpose(2, 1, 0, 3).reshape(2, rows, cols)
    return back[0], back[1]


def gather_weights(w_first, w_second):
    halves = lax.axis_size("zh")
    h = lax.axis_index("zh")
    shards_n = lax.axis_size(NARROW)
    r1 = w_first.shape[0] // halves
    r2 = w_second.shape[0] // halves
    mine = jnp.concatenate(
        [
            lax.dynamic_slice_in_dim(w_first, h * r1, r1, axis=0),
            lax.dynamic_slice_in_dim(w_second, h * r2, r2, axis=0),
        ],
        axis=0,
    )
    got = lax.all_gather(mine, ("zh",) + NARROW, axis=0, tiled=False)
    got = got.reshape(halves, shards_n, r1 + r2, got.shape[-1]).transpose(1, 0, 2, 3)
    first = got[:, :, :r1].reshape(shards_n * halves * r1, -1)
    second = got[:, :, r1:].reshape(shards_n * halves * r2, -1)
    return first, second


def shards(
    tile_pool,
    batch_index,
    pair_label,
    w_first,
    w_second,
    m_first,
    m_second,
    v_first,
    v_second,
    mom_first,
    mom_second,
):
    inputs = jnp.take(tile_pool[0], batch_index[0], axis=0)
    partner = pair_label[0]
    scale_one = 1.0 / math.sqrt(PIX)
    scale_two = 1.0 / math.sqrt(MID)
    first_whole, second_whole = gather_weights(w_first, w_second)
    hidden = jnp.dot(inputs, first_whole, preferred_element_type=jnp.float32) * scale_one
    active_full, gelu_back = jax.vjp(jax.nn.gelu, hidden)
    active = active_full.astype(jnp.bfloat16)
    embedded = jnp.dot(active, second_whole, preferred_element_type=jnp.float32) * scale_two
    embed_half = embed_gradient(embedded, partner)
    grad_second = lax.psum_scatter(
        (scale_two * jnp.dot(active.T, embed_half, preferred_element_type=jnp.float32)).astype(
            jnp.bfloat16
        ),
        NARROW,
        scatter_dimension=0,
        tiled=True,
    ).astype(jnp.float32)
    delta_second = adam_delta(grad_second, m_second[0], v_second[0], w_second)
    active_grad = scale_two * jnp.dot(
        embed_half, second_whole.T, preferred_element_type=jnp.float32
    )
    hidden_half = gelu_back(active_grad)[0].astype(jnp.bfloat16)
    grad_first = lax.psum_scatter(
        (scale_one * jnp.dot(inputs.T, hidden_half, preferred_element_type=jnp.float32)).astype(
            jnp.bfloat16
        ),
        NARROW,
        scatter_dimension=0,
        tiled=True,
    ).astype(jnp.float32)
    delta_first = adam_delta(grad_first, m_first[0], v_first[0], w_first)
    rows_first = delta_first.shape[0]
    new_w, vel = wide_mean_update(
        jnp.concatenate([delta_first, delta_second], axis=0),
        jnp.concatenate([mom_first, mom_second], axis=0),
        jnp.concatenate([w_first, w_second], axis=0),
    )
    return (new_w[:rows_first], new_w[rows_first:], vel[:rows_first], vel[rows_first:])


def solution(mesh):
    zh, y, x = 2, 4, 4
    devices = np.asarray(mesh.devices)
    wide, narrow = devices.shape
    sub = Mesh(devices.reshape(zh, y, x, narrow // 2, 2), WIDE + NARROW)
    site = P(WIDE, NARROW, None)
    rows = P(NARROW, None)
    return jax.shard_map(
        shards,
        mesh=sub,
        in_specs=(site, P(WIDE, NARROW), P(WIDE, NARROW), rows, rows, site, site, site, site, rows, rows),
        out_specs=(rows, rows, rows, rows),
        check_vma=False,
    )
```

```python
import math

import jax
import jax.numpy as jnp
import numpy as np
from jax import lax
from jax.sharding import Mesh
from jax.sharding import PartitionSpec as P

PIX = 768
MID = 2048
OUT = 2048


logit_scale = 1.0 / 0.07
rate_inner = 0.2
weight_decay = 0.1
beta_first = 0.9
beta_second = 0.95
adam_eps = 1e-08
rate_outer = 0.7
momentum_coef = 0.9

WIDE = ("zh", "y", "x")
NARROW = ("zl", "c")


def adam_delta(grads, first_moment, second_moment, weights):
    moment_one = beta_first * first_moment.astype(jnp.float32) + (1.0 - beta_first) * grads
    moment_two = (
        beta_second * second_moment.astype(jnp.float32) + (1.0 - beta_second) * grads * grads
    )
    return rate_inner * (
        moment_one / (jnp.sqrt(moment_two) + adam_eps) + weight_decay * weights.astype(jnp.float32)
    )


def outer_update(delta, momentum, weights):
    velocity = momentum_coef * momentum.astype(jnp.float32) + delta
    updated = weights.astype(jnp.float32) - rate_outer * (delta + momentum_coef * velocity)
    return (updated.astype(jnp.bfloat16), velocity.astype(jnp.bfloat16))


def embed_gradient(embedded, partner):
    inverse = lax.rsqrt(jnp.sum(embedded * embedded, axis=1, keepdims=True) + OUT * 1e-06)
    unit_rows = embedded * inverse
    unit_half = unit_rows.astype(jnp.bfloat16)
    scores = logit_scale * jnp.dot(unit_half, unit_half.T, preferred_element_type=jnp.float32)
    positions = jnp.arange(embedded.shape[0], dtype=jnp.int32)
    diagonal = positions[:, None] == positions[None, :]
    scores = jnp.where(diagonal, -1e30, scores)
    highest = jnp.max(scores, axis=1, keepdims=True)
    powers = jnp.exp(scores - highest)
    softmax_rows = powers / jnp.sum(powers, axis=1, keepdims=True)
    target = (partner[:, None] == positions[None, :]).astype(jnp.float32)
    score_grad = softmax_rows - target
    paired = (score_grad + score_grad.T).astype(jnp.bfloat16)
    unit_grad = logit_scale * jnp.dot(paired, unit_half, preferred_element_type=jnp.float32)
    embed_grad = inverse * (
        unit_grad - unit_rows * jnp.sum(unit_rows * unit_grad, axis=1, keepdims=True)
    )
    return embed_grad.astype(jnp.bfloat16)


def wide_mean_update(delta, momentum, weights):
    plane = ("y", "x")
    n_plane = lax.axis_size(plane)
    n_half = lax.axis_size("zh")
    sites = n_plane * n_half
    rows, cols = delta.shape
    p1 = cols // n_plane
    p2 = p1 // n_half
    got = lax.all_to_all(delta, plane, 1, 0, tiled=True)
    part = jnp.sum(got.reshape(n_plane, rows, p1), axis=0)
    got = lax.all_to_all(part, "zh", 1, 0, tiled=True)
    mean = jnp.sum(got.reshape(n_half, rows, p2), axis=0) / sites
    start = lax.axis_index(plane) * p1 + lax.axis_index("zh") * p2
    mom_piece = lax.dynamic_slice_in_dim(momentum, start, p2, axis=1)
    w_piece = lax.dynamic_slice_in_dim(weights, start, p2, axis=1)
    new_piece, vel_piece = outer_update(mean, mom_piece, w_piece)
    both = jnp.stack([new_piece, vel_piece], axis=0)
    back = lax.all_to_all(jnp.broadcast_to(both[None], (n_half,) + both.shape), "zh", 0, 0, tiled=True)
    back = back.transpose(1, 2, 0, 3).reshape(2, rows, p1)
    back = lax.all_to_all(jnp.broadcast_to(back[None], (n_plane,) + back.shape), plane, 0, 0, tiled=True)
    back = back.transpose(1, 2, 0, 3).reshape(2, rows, cols)
    return back[0], back[1]


def gather_weights(w_first, w_second):
    halves = lax.axis_size("zh")
    h = lax.axis_index("zh")
    shards_n = lax.axis_size(NARROW)
    r1 = w_first.shape[0] // halves
    r2 = w_second.shape[0] // halves
    mine = jnp.concatenate(
        [
            lax.dynamic_slice_in_dim(w_first, h * r1, r1, axis=0),
            lax.dynamic_slice_in_dim(w_second, h * r2, r2, axis=0),
        ],
        axis=0,
    )
    got = lax.all_gather(mine, ("zh",) + NARROW, axis=0, tiled=False)
    got = got.reshape(halves, shards_n, r1 + r2, got.shape[-1]).transpose(1, 0, 2, 3)
    first = got[:, :, :r1].reshape(shards_n * halves * r1, -1)
    second = got[:, :, r1:].reshape(shards_n * halves * r2, -1)
    return first, second


def shards(
    tile_pool,
    batch_index,
    pair_label,
    w_first,
    w_second,
    m_first,
    m_second,
    v_first,
    v_second,
    mom_first,
    mom_second,
):
    inputs = jnp.take(tile_pool[0], batch_index[0], axis=0)
    partner = pair_label[0]
    scale_one = 1.0 / math.sqrt(PIX)
    scale_two = 1.0 / math.sqrt(MID)
    first_whole, second_whole = gather_weights(w_first, w_second)
    hidden = jnp.dot(inputs, first_whole, preferred_element_type=jnp.float32) * scale_one
    active_full, gelu_back = jax.vjp(jax.nn.gelu, hidden)
    active = active_full.astype(jnp.bfloat16)
    embedded = jnp.dot(active, second_whole, preferred_element_type=jnp.float32) * scale_two
    embed_half = embed_gradient(embedded, partner)
    grad_second = lax.psum_scatter(
        (scale_two * jnp.dot(active.T, embed_half, preferred_element_type=jnp.float32)).astype(
            jnp.bfloat16
        ),
        NARROW,
        scatter_dimension=0,
        tiled=True,
    ).astype(jnp.float32)
    delta_second = adam_delta(grad_second, m_second[0], v_second[0], w_second)
    active_grad = scale_two * jnp.dot(
        embed_half, second_whole.T, preferred_element_type=jnp.float32
    )
    hidden_half = gelu_back(active_grad)[0].astype(jnp.bfloat16)
    grad_first = lax.psum_scatter(
        (scale_one * jnp.dot(inputs.T, hidden_half, preferred_element_type=jnp.float32)).astype(
            jnp.bfloat16
        ),
        NARROW,
        scatter_dimension=0,
        tiled=True,
    ).astype(jnp.float32)
    delta_first = adam_delta(grad_first, m_first[0], v_first[0], w_first)
    rows_first = delta_first.shape[0]
    new_w, vel = wide_mean_update(
        jnp.concatenate([delta_first, delta_second], axis=0),
        jnp.concatenate([mom_first, mom_second], axis=0),
        jnp.concatenate([w_first, w_second], axis=0),
    )
    return (new_w[:rows_first], new_w[rows_first:], vel[:rows_first], vel[rows_first:])


def solution(mesh):
    zh, y, x = 2, 4, 4
    devices = np.asarray(mesh.devices)
    wide, narrow = devices.shape
    sub = Mesh(devices.reshape(zh, y, x, narrow // 2, 2), WIDE + NARROW)
    site = P(WIDE, NARROW, None)
    rows = P(NARROW, None)
    return jax.shard_map(
        shards,
        mesh=sub,
        in_specs=(site, P(WIDE, NARROW), P(WIDE, NARROW), rows, rows, site, site, site, site, rows, rows),
        out_specs=(rows, rows, rows, rows),
        check_vma=False,
    )
```

```python
import math

import jax
import jax.numpy as jnp
import numpy as np
from jax import lax
from jax.sharding import Mesh
from jax.sharding import PartitionSpec as P

PIX = 768
MID = 2048
OUT = 2048


logit_scale = 1.0 / 0.07
rate_inner = 0.2
weight_decay = 0.1
beta_first = 0.9
beta_second = 0.95
adam_eps = 1e-08
rate_outer = 0.7
momentum_coef = 0.9

WIDE = ("zh", "y", "x")
NARROW = ("zl", "c")


def adam_delta(grads, first_moment, second_moment, weights):
    moment_one = beta_first * first_moment.astype(jnp.float32) + (1.0 - beta_first) * grads
    moment_two = (
        beta_second * second_moment.astype(jnp.float32) + (1.0 - beta_second) * grads * grads
    )
    return rate_inner * (
        moment_one / (jnp.sqrt(moment_two) + adam_eps) + weight_decay * weights.astype(jnp.float32)
    )


def outer_update(delta, momentum, weights):
    velocity = momentum_coef * momentum.astype(jnp.float32) + delta
    updated = weights.astype(jnp.float32) - rate_outer * (delta + momentum_coef * velocity)
    return (updated.astype(jnp.bfloat16), velocity.astype(jnp.bfloat16))


def embed_gradient(embedded, partner):
    inverse = lax.rsqrt(jnp.sum(embedded * embedded, axis=1, keepdims=True) + OUT * 1e-06)
    unit_rows = embedded * inverse
    unit_half = unit_rows.astype(jnp.bfloat16)
    scores = logit_scale * jnp.dot(unit_half, unit_half.T, preferred_element_type=jnp.float32)
    positions = jnp.arange(embedded.shape[0], dtype=jnp.int32)
    diagonal = positions[:, None] == positions[None, :]
    scores = jnp.where(diagonal, -1e30, scores)
    highest = jnp.max(scores, axis=1, keepdims=True)
    powers = jnp.exp(scores - highest)
    softmax_rows = powers / jnp.sum(powers, axis=1, keepdims=True)
    target = (partner[:, None] == positions[None, :]).astype(jnp.float32)
    score_grad = softmax_rows - target
    paired = (score_grad + score_grad.T).astype(jnp.bfloat16)
    unit_grad = logit_scale * jnp.dot(paired, unit_half, preferred_element_type=jnp.float32)
    embed_grad = inverse * (
        unit_grad - unit_rows * jnp.sum(unit_rows * unit_grad, axis=1, keepdims=True)
    )
    return embed_grad.astype(jnp.bfloat16)


def wide_mean_update(delta, momentum, weights):
    plane = ("y", "x")
    n_plane = lax.axis_size(plane)
    n_half = lax.axis_size("zh")
    sites = n_plane * n_half
    rows, cols = delta.shape
    p1 = cols // n_plane
    p2 = p1 // n_half
    got = lax.all_to_all(delta, plane, 1, 0, tiled=True)
    part = jnp.sum(got.reshape(n_plane, rows, p1), axis=0)
    got = lax.all_to_all(part, "zh", 1, 0, tiled=True)
    mean = jnp.sum(got.reshape(n_half, rows, p2), axis=0) / sites
    start = lax.axis_index(plane) * p1 + lax.axis_index("zh") * p2
    mom_piece = lax.dynamic_slice_in_dim(momentum, start, p2, axis=1)
    w_piece = lax.dynamic_slice_in_dim(weights, start, p2, axis=1)
    new_piece, vel_piece = outer_update(mean, mom_piece, w_piece)
    both = jnp.stack([new_piece, vel_piece], axis=0)
    back = lax.all_to_all(jnp.broadcast_to(both[None], (n_half,) + both.shape), "zh", 0, 0, tiled=True)
    back = back.transpose(1, 2, 0, 3).reshape(2, rows, p1)
    back = lax.all_to_all(jnp.broadcast_to(back[None], (n_plane,) + back.shape), plane, 0, 0, tiled=True)
    back = back.transpose(1, 2, 0, 3).reshape(2, rows, cols)
    return back[0], back[1]


def gather_weights(w_first, w_second):
    halves = lax.axis_size("zh")
    h = lax.axis_index("zh")
    shards_n = lax.axis_size(NARROW)
    r1 = w_first.shape[0] // halves
    r2 = w_second.shape[0] // halves
    mine = jnp.concatenate(
        [
            lax.dynamic_slice_in_dim(w_first, h * r1, r1, axis=0),
            lax.dynamic_slice_in_dim(w_second, h * r2, r2, axis=0),
        ],
        axis=0,
    )
    got = lax.all_gather(mine, ("zh",) + NARROW, axis=0, tiled=False)
    got = got.reshape(halves, shards_n, r1 + r2, got.shape[-1]).transpose(1, 0, 2, 3)
    first = got[:, :, :r1].reshape(shards_n * halves * r1, -1)
    second = got[:, :, r1:].reshape(shards_n * halves * r2, -1)
    return first, second


def shards(
    tile_pool,
    batch_index,
    pair_label,
    w_first,
    w_second,
    m_first,
    m_second,
    v_first,
    v_second,
    mom_first,
    mom_second,
):
    inputs = jnp.take(tile_pool[0], batch_index[0], axis=0)
    partner = pair_label[0]
    scale_one = 1.0 / math.sqrt(PIX)
    scale_two = 1.0 / math.sqrt(MID)
    first_whole, second_whole = gather_weights(w_first, w_second)
    hidden = jnp.dot(inputs, first_whole, preferred_element_type=jnp.float32) * scale_one
    active_full, gelu_back = jax.vjp(jax.nn.gelu, hidden)
    active = active_full.astype(jnp.bfloat16)
    embedded = jnp.dot(active, second_whole, preferred_element_type=jnp.float32) * scale_two
    embed_half = embed_gradient(embedded, partner)
    grad_second = lax.psum_scatter(
        (scale_two * jnp.dot(active.T, embed_half, preferred_element_type=jnp.float32)).astype(
            jnp.bfloat16
        ),
        NARROW,
        scatter_dimension=0,
        tiled=True,
    ).astype(jnp.float32)
    active_grad = scale_two * jnp.dot(
        embed_half, second_whole.T, preferred_element_type=jnp.float32
    )
    hidden_half = gelu_back(active_grad)[0].astype(jnp.bfloat16)
    term_first = (
        scale_one * jnp.dot(inputs.T, hidden_half, preferred_element_type=jnp.float32)
    ).astype(jnp.bfloat16)
    term_first, grad_second = lax.optimization_barrier((term_first, grad_second))
    delta_second = adam_delta(grad_second, m_second[0], v_second[0], w_second)
    new_second, vel_second = wide_mean_update(delta_second, mom_second, w_second)
    grad_first = lax.psum_scatter(
        term_first, NARROW, scatter_dimension=0, tiled=True
    ).astype(jnp.float32)
    delta_first = adam_delta(grad_first, m_first[0], v_first[0], w_first)
    new_first, vel_first = wide_mean_update(delta_first, mom_first, w_first)
    return (new_first, new_second, vel_first, vel_second)


def solution(mesh):
    zh, y, x = 2, 4, 4
    devices = np.asarray(mesh.devices)
    wide, narrow = devices.shape
    sub = Mesh(devices.reshape(zh, y, x, narrow // 2, 2), WIDE + NARROW)
    site = P(WIDE, NARROW, None)
    rows = P(NARROW, None)
    return jax.shard_map(
        shards,
        mesh=sub,
        in_specs=(site, P(WIDE, NARROW), P(WIDE, NARROW), rows, rows, site, site, site, site, rows, rows),
        out_specs=(rows, rows, rows, rows),
        check_vma=False,
    )
```

```python
import math

import jax
import jax.numpy as jnp
import numpy as np
from jax import lax
from jax.sharding import Mesh
from jax.sharding import PartitionSpec as P

PIX = 768
MID = 2048
OUT = 2048


logit_scale = 1.0 / 0.07
rate_inner = 0.2
weight_decay = 0.1
beta_first = 0.9
beta_second = 0.95
adam_eps = 1e-08
rate_outer = 0.7
momentum_coef = 0.9

WIDE = ("zh", "y", "x")
NARROW = ("zl", "c")


def adam_delta(grads, first_moment, second_moment, weights):
    moment_one = beta_first * first_moment.astype(jnp.float32) + (1.0 - beta_first) * grads
    moment_two = (
        beta_second * second_moment.astype(jnp.float32) + (1.0 - beta_second) * grads * grads
    )
    return rate_inner * (
        moment_one / (jnp.sqrt(moment_two) + adam_eps) + weight_decay * weights.astype(jnp.float32)
    )


def outer_update(delta, momentum, weights):
    velocity = momentum_coef * momentum.astype(jnp.float32) + delta
    updated = weights.astype(jnp.float32) - rate_outer * (delta + momentum_coef * velocity)
    return (updated.astype(jnp.bfloat16), velocity.astype(jnp.bfloat16))


def embed_gradient(embedded, partner):
    inverse = lax.rsqrt(jnp.sum(embedded * embedded, axis=1, keepdims=True) + OUT * 1e-06)
    unit_rows = embedded * inverse
    unit_half = unit_rows.astype(jnp.bfloat16)
    scores = logit_scale * jnp.dot(unit_half, unit_half.T, preferred_element_type=jnp.float32)
    positions = jnp.arange(embedded.shape[0], dtype=jnp.int32)
    diagonal = positions[:, None] == positions[None, :]
    scores = jnp.where(diagonal, -1e30, scores)
    highest = jnp.max(scores, axis=1, keepdims=True)
    powers = jnp.exp(scores - highest)
    softmax_rows = powers / jnp.sum(powers, axis=1, keepdims=True)
    target = (partner[:, None] == positions[None, :]).astype(jnp.float32)
    score_grad = softmax_rows - target
    paired = (score_grad + score_grad.T).astype(jnp.bfloat16)
    unit_grad = logit_scale * jnp.dot(paired, unit_half, preferred_element_type=jnp.float32)
    embed_grad = inverse * (
        unit_grad - unit_rows * jnp.sum(unit_rows * unit_grad, axis=1, keepdims=True)
    )
    return embed_grad.astype(jnp.bfloat16)


def wide_mean_update(delta, momentum, weights):
    plane = ("y", "x")
    n_plane = lax.axis_size(plane)
    n_half = lax.axis_size("zh")
    sites = n_plane * n_half
    rows, cols = delta.shape
    p1 = cols // n_plane
    p2 = p1 // n_half
    got = lax.all_to_all(delta, plane, 1, 0, tiled=True)
    part = jnp.sum(got.reshape(n_plane, rows, p1), axis=0)
    got = lax.all_to_all(part, "zh", 1, 0, tiled=True)
    mean = jnp.sum(got.reshape(n_half, rows, p2), axis=0) / sites
    start = lax.axis_index(plane) * p1 + lax.axis_index("zh") * p2
    mom_piece = lax.dynamic_slice_in_dim(momentum, start, p2, axis=1)
    w_piece = lax.dynamic_slice_in_dim(weights, start, p2, axis=1)
    new_piece, vel_piece = outer_update(mean, mom_piece, w_piece)
    both = jnp.stack([new_piece, vel_piece], axis=0)
    back = lax.all_to_all(jnp.broadcast_to(both[None], (n_half,) + both.shape), "zh", 0, 0, tiled=True)
    back = back.transpose(1, 2, 0, 3).reshape(2, rows, p1)
    back = lax.all_to_all(jnp.broadcast_to(back[None], (n_plane,) + back.shape), plane, 0, 0, tiled=True)
    back = back.transpose(1, 2, 0, 3).reshape(2, rows, cols)
    return back[0], back[1]


def gather_weights(w_first, w_second):
    halves = lax.axis_size("zh")
    h = lax.axis_index("zh")
    shards_n = lax.axis_size(NARROW)
    r1 = w_first.shape[0] // halves
    r2 = w_second.shape[0] // halves
    mine = jnp.concatenate(
        [
            lax.dynamic_slice_in_dim(w_first, h * r1, r1, axis=0),
            lax.dynamic_slice_in_dim(w_second, h * r2, r2, axis=0),
        ],
        axis=0,
    )
    got = lax.all_gather(mine, ("zh",) + NARROW, axis=0, tiled=False)
    got = got.reshape(halves, shards_n, r1 + r2, got.shape[-1])
    return got[:, :, :r1], got[:, :, r1:]


def split_rows(x, like):
    halves, shards_n, r = like.shape[:3]
    return x.reshape(x.shape[0], shards_n, halves, r)


def shards(
    tile_pool,
    batch_index,
    pair_label,
    w_first,
    w_second,
    m_first,
    m_second,
    v_first,
    v_second,
    mom_first,
    mom_second,
):
    inputs = jnp.take(tile_pool[0], batch_index[0], axis=0)
    partner = pair_label[0]
    scale_one = 1.0 / math.sqrt(PIX)
    scale_two = 1.0 / math.sqrt(MID)
    first_whole, second_whole = gather_weights(w_first, w_second)
    hidden = (
        jnp.einsum("bnhr,hnrc->bc", split_rows(inputs, first_whole), first_whole,
                   preferred_element_type=jnp.float32)
        * scale_one
    )
    active_full, gelu_back = jax.vjp(jax.nn.gelu, hidden)
    active = active_full.astype(jnp.bfloat16)
    embedded = (
        jnp.einsum("bnhr,hnrc->bc", split_rows(active, second_whole), second_whole,
                   preferred_element_type=jnp.float32)
        * scale_two
    )
    embed_half = embed_gradient(embedded, partner)
    grad_second = lax.psum_scatter(
        (scale_two * jnp.dot(active.T, embed_half, preferred_element_type=jnp.float32)).astype(
            jnp.bfloat16
        ),
        NARROW,
        scatter_dimension=0,
        tiled=True,
    ).astype(jnp.float32)
    active_grad = scale_two * jnp.einsum(
        "bc,hnrc->bnhr", embed_half, second_whole, preferred_element_type=jnp.float32
    ).reshape(active.shape)
    hidden_half = gelu_back(active_grad)[0].astype(jnp.bfloat16)
    term_first = (
        scale_one * jnp.dot(inputs.T, hidden_half, preferred_element_type=jnp.float32)
    ).astype(jnp.bfloat16)
    term_first, grad_second = lax.optimization_barrier((term_first, grad_second))
    delta_second = adam_delta(grad_second, m_second[0], v_second[0], w_second)
    new_second, vel_second = wide_mean_update(delta_second, mom_second, w_second)
    grad_first = lax.psum_scatter(
        term_first, NARROW, scatter_dimension=0, tiled=True
    ).astype(jnp.float32)
    delta_first = adam_delta(grad_first, m_first[0], v_first[0], w_first)
    new_first, vel_first = wide_mean_update(delta_first, mom_first, w_first)
    return (new_first, new_second, vel_first, vel_second)


def solution(mesh):
    zh, y, x = 2, 4, 4
    devices = np.asarray(mesh.devices)
    wide, narrow = devices.shape
    sub = Mesh(devices.reshape(zh, y, x, narrow // 2, 2), WIDE + NARROW)
    site = P(WIDE, NARROW, None)
    rows = P(NARROW, None)
    return jax.shard_map(
        shards,
        mesh=sub,
        in_specs=(site, P(WIDE, NARROW), P(WIDE, NARROW), rows, rows, site, site, site, site, rows, rows),
        out_specs=(rows, rows, rows, rows),
        check_vma=False,
    )
```

```python
import math

import jax
import jax.numpy as jnp
import numpy as np
from jax import lax
from jax.sharding import Mesh
from jax.sharding import PartitionSpec as P

PIX = 768
MID = 2048
OUT = 2048


logit_scale = 1.0 / 0.07
rate_inner = 0.2
weight_decay = 0.1
beta_first = 0.9
beta_second = 0.95
adam_eps = 1e-08
rate_outer = 0.7
momentum_coef = 0.9

WIDE = ("zh", "y", "x")
NARROW = ("zl", "c")


def adam_delta(grads, first_moment, second_moment, weights):
    moment_one = beta_first * first_moment.astype(jnp.float32) + (1.0 - beta_first) * grads
    moment_two = (
        beta_second * second_moment.astype(jnp.float32) + (1.0 - beta_second) * grads * grads
    )
    return rate_inner * (
        moment_one / (jnp.sqrt(moment_two) + adam_eps) + weight_decay * weights.astype(jnp.float32)
    )


def outer_update(delta, momentum, weights):
    velocity = momentum_coef * momentum.astype(jnp.float32) + delta
    updated = weights.astype(jnp.float32) - rate_outer * (delta + momentum_coef * velocity)
    return (updated.astype(jnp.bfloat16), velocity.astype(jnp.bfloat16))


def embed_gradient(embedded, partner):
    inverse = lax.rsqrt(jnp.sum(embedded * embedded, axis=1, keepdims=True) + OUT * 1e-06)
    unit_rows = embedded * inverse
    unit_half = unit_rows.astype(jnp.bfloat16)
    scores = logit_scale * jnp.dot(unit_half, unit_half.T, preferred_element_type=jnp.float32)
    positions = jnp.arange(embedded.shape[0], dtype=jnp.int32)
    diagonal = positions[:, None] == positions[None, :]
    scores = jnp.where(diagonal, -1e30, scores)
    highest = jnp.max(scores, axis=1, keepdims=True)
    powers = jnp.exp(scores - highest)
    softmax_rows = powers / jnp.sum(powers, axis=1, keepdims=True)
    target = (partner[:, None] == positions[None, :]).astype(jnp.float32)
    score_grad = softmax_rows - target
    paired = (score_grad + score_grad.T).astype(jnp.bfloat16)
    unit_grad = logit_scale * jnp.dot(paired, unit_half, preferred_element_type=jnp.float32)
    embed_grad = inverse * (
        unit_grad - unit_rows * jnp.sum(unit_rows * unit_grad, axis=1, keepdims=True)
    )
    return embed_grad.astype(jnp.bfloat16)


def plane_sum(delta):
    plane = ("y", "x")
    n_plane = lax.axis_size(plane)
    rows, cols = delta.shape
    got = lax.all_to_all(delta, plane, 1, 0, tiled=True)
    return jnp.sum(got.reshape(n_plane, rows, cols // n_plane), axis=0)


def wide_mean_update(delta, momentum, weights, part=None):
    plane = ("y", "x")
    n_plane = lax.axis_size(plane)
    n_half = lax.axis_size("zh")
    sites = n_plane * n_half
    rows, cols = delta.shape
    p1 = cols // n_plane
    p2 = p1 // n_half
    part = plane_sum(delta) if part is None else part
    got = lax.all_to_all(part, "zh", 1, 0, tiled=True)
    mean = jnp.sum(got.reshape(n_half, rows, p2), axis=0) / sites
    start = lax.axis_index(plane) * p1 + lax.axis_index("zh") * p2
    mom_piece = lax.dynamic_slice_in_dim(momentum, start, p2, axis=1)
    w_piece = lax.dynamic_slice_in_dim(weights, start, p2, axis=1)
    new_piece, vel_piece = outer_update(mean, mom_piece, w_piece)
    both = jnp.stack([new_piece, vel_piece], axis=0)
    back = lax.all_to_all(jnp.broadcast_to(both[None], (n_half,) + both.shape), "zh", 0, 0, tiled=True)
    back = back.transpose(1, 2, 0, 3).reshape(2, rows, p1)
    back = lax.all_to_all(jnp.broadcast_to(back[None], (n_plane,) + back.shape), plane, 0, 0, tiled=True)
    back = back.transpose(1, 2, 0, 3).reshape(2, rows, cols)
    return back[0], back[1]


def gather_weights(w_first, w_second):
    halves = lax.axis_size("zh")
    h = lax.axis_index("zh")
    shards_n = lax.axis_size(NARROW)
    r1 = w_first.shape[0] // halves
    r2 = w_second.shape[0] // halves
    mine = jnp.concatenate(
        [
            lax.dynamic_slice_in_dim(w_first, h * r1, r1, axis=0),
            lax.dynamic_slice_in_dim(w_second, h * r2, r2, axis=0),
        ],
        axis=0,
    )
    got = lax.all_gather(mine, ("zh",) + NARROW, axis=0, tiled=False)
    got = got.reshape(halves, shards_n, r1 + r2, got.shape[-1])
    return got[:, :, :r1], got[:, :, r1:]


def split_rows(x, like):
    halves, shards_n, r = like.shape[:3]
    return x.reshape(x.shape[0], shards_n, halves, r)


def shards(
    tile_pool,
    batch_index,
    pair_label,
    w_first,
    w_second,
    m_first,
    m_second,
    v_first,
    v_second,
    mom_first,
    mom_second,
):
    inputs = jnp.take(tile_pool[0], batch_index[0], axis=0)
    partner = pair_label[0]
    scale_one = 1.0 / math.sqrt(PIX)
    scale_two = 1.0 / math.sqrt(MID)
    first_whole, second_whole = gather_weights(w_first, w_second)
    hidden = (
        jnp.einsum("bnhr,hnrc->bc", split_rows(inputs, first_whole), first_whole,
                   preferred_element_type=jnp.float32)
        * scale_one
    )
    active_full, gelu_back = jax.vjp(jax.nn.gelu, hidden)
    active = active_full.astype(jnp.bfloat16)
    embedded = (
        jnp.einsum("bnhr,hnrc->bc", split_rows(active, second_whole), second_whole,
                   preferred_element_type=jnp.float32)
        * scale_two
    )
    embed_half = embed_gradient(embedded, partner)
    term_second = (
        scale_two * jnp.dot(active.T, embed_half, preferred_element_type=jnp.float32)
    ).astype(jnp.bfloat16)
    cols = term_second.shape[1] // 2
    first_part, second_part = term_second[:, :cols], term_second[:, cols:]
    grad_a = lax.psum_scatter(first_part, NARROW, scatter_dimension=0, tiled=True)
    active_grad = scale_two * jnp.einsum(
        "bc,hnrc->bnhr", embed_half, second_whole, preferred_element_type=jnp.float32
    ).reshape(active.shape)
    hidden_half = gelu_back(active_grad)[0].astype(jnp.bfloat16)
    term_first = (
        scale_one * jnp.dot(inputs.T, hidden_half, preferred_element_type=jnp.float32)
    ).astype(jnp.bfloat16)
    left = slice(0, cols)
    right = slice(cols, 2 * cols)
    delta_a = adam_delta(
        grad_a.astype(jnp.float32), m_second[0][:, left], v_second[0][:, left], w_second[:, left]
    )
    plane_a = plane_sum(delta_a)
    second_part, plane_a = lax.optimization_barrier((second_part, plane_a))
    grad_b = lax.psum_scatter(second_part, NARROW, scatter_dimension=0, tiled=True)
    out_a = wide_mean_update(delta_a, mom_second[:, left], w_second[:, left], plane_a)
    term_first, grad_b = lax.optimization_barrier((term_first, grad_b))
    delta_b = adam_delta(
        grad_b.astype(jnp.float32), m_second[0][:, right], v_second[0][:, right], w_second[:, right]
    )
    out_b = wide_mean_update(delta_b, mom_second[:, right], w_second[:, right])
    new_second = jnp.concatenate([out_a[0], out_b[0]], axis=1)
    vel_second = jnp.concatenate([out_a[1], out_b[1]], axis=1)
    grad_first = lax.psum_scatter(
        term_first, NARROW, scatter_dimension=0, tiled=True
    ).astype(jnp.float32)
    delta_first = adam_delta(grad_first, m_first[0], v_first[0], w_first)
    new_first, vel_first = wide_mean_update(delta_first, mom_first, w_first)
    return (new_first, new_second, vel_first, vel_second)


def solution(mesh):
    zh, y, x = 2, 4, 4
    devices = np.asarray(mesh.devices)
    wide, narrow = devices.shape
    sub = Mesh(devices.reshape(zh, y, x, narrow // 2, 2), WIDE + NARROW)
    site = P(WIDE, NARROW, None)
    rows = P(NARROW, None)
    return jax.shard_map(
        shards,
        mesh=sub,
        in_specs=(site, P(WIDE, NARROW), P(WIDE, NARROW), rows, rows, site, site, site, site, rows, rows),
        out_specs=(rows, rows, rows, rows),
        check_vma=False,
    )
```

```python
import math

import jax
import jax.numpy as jnp
import numpy as np
from jax import lax
from jax.sharding import Mesh
from jax.sharding import PartitionSpec as P

PIX = 768
MID = 2048
OUT = 2048


logit_scale = 1.0 / 0.07
rate_inner = 0.2
weight_decay = 0.1
beta_first = 0.9
beta_second = 0.95
adam_eps = 1e-08
rate_outer = 0.7
momentum_coef = 0.9

WIDE = ("zh", "y", "x")
NARROW = ("zl", "c")


def adam_delta(grads, first_moment, second_moment, weights):
    moment_one = beta_first * first_moment.astype(jnp.float32) + (1.0 - beta_first) * grads
    moment_two = (
        beta_second * second_moment.astype(jnp.float32) + (1.0 - beta_second) * grads * grads
    )
    return rate_inner * (
        moment_one / (jnp.sqrt(moment_two) + adam_eps) + weight_decay * weights.astype(jnp.float32)
    )


def outer_update(delta, momentum, weights):
    velocity = momentum_coef * momentum.astype(jnp.float32) + delta
    updated = weights.astype(jnp.float32) - rate_outer * (delta + momentum_coef * velocity)
    return (updated.astype(jnp.bfloat16), velocity.astype(jnp.bfloat16))


def embed_gradient(embedded, partner):
    inverse = lax.rsqrt(jnp.sum(embedded * embedded, axis=1, keepdims=True) + OUT * 1e-06)
    unit_rows = embedded * inverse
    unit_half = unit_rows.astype(jnp.bfloat16)
    scores = logit_scale * jnp.dot(unit_half, unit_half.T, preferred_element_type=jnp.float32)
    positions = jnp.arange(embedded.shape[0], dtype=jnp.int32)
    diagonal = positions[:, None] == positions[None, :]
    scores = jnp.where(diagonal, -1e30, scores)
    highest = jnp.max(scores, axis=1, keepdims=True)
    powers = jnp.exp(scores - highest)
    softmax_rows = powers / jnp.sum(powers, axis=1, keepdims=True)
    target = (partner[:, None] == positions[None, :]).astype(jnp.float32)
    score_grad = softmax_rows - target
    paired = (score_grad + score_grad.T).astype(jnp.bfloat16)
    unit_grad = logit_scale * jnp.dot(paired, unit_half, preferred_element_type=jnp.float32)
    embed_grad = inverse * (
        unit_grad - unit_rows * jnp.sum(unit_rows * unit_grad, axis=1, keepdims=True)
    )
    return embed_grad.astype(jnp.bfloat16)


def plane_sum(delta):
    plane = ("y", "x")
    n_plane = lax.axis_size(plane)
    rows, cols = delta.shape
    got = lax.all_to_all(delta, plane, 1, 0, tiled=True)
    return jnp.sum(got.reshape(n_plane, rows, cols // n_plane), axis=0)


def wide_mean_update(delta, momentum, weights, part=None):
    plane = ("y", "x")
    n_plane = lax.axis_size(plane)
    n_half = lax.axis_size("zh")
    sites = n_plane * n_half
    rows, cols = momentum.shape
    p1 = cols // n_plane
    p2 = p1 // n_half
    part = plane_sum(delta) if part is None else part
    got = lax.all_to_all(part, "zh", 1, 0, tiled=True)
    mean = jnp.sum(got.reshape(n_half, rows, p2), axis=0) / sites
    start = lax.axis_index(plane) * p1 + lax.axis_index("zh") * p2
    mom_piece = lax.dynamic_slice_in_dim(momentum, start, p2, axis=1)
    w_piece = lax.dynamic_slice_in_dim(weights, start, p2, axis=1)
    new_piece, vel_piece = outer_update(mean, mom_piece, w_piece)
    both = jnp.stack([new_piece, vel_piece], axis=0)
    back = lax.all_to_all(jnp.broadcast_to(both[None], (n_half,) + both.shape), "zh", 0, 0, tiled=True)
    back = back.transpose(1, 2, 0, 3).reshape(2, rows, p1)
    back = lax.all_to_all(jnp.broadcast_to(back[None], (n_plane,) + back.shape), plane, 0, 0, tiled=True)
    back = back.transpose(1, 2, 0, 3).reshape(2, rows, cols)
    return back[0], back[1]


def gather_weights(w_first, w_second):
    halves = lax.axis_size("zh")
    h = lax.axis_index("zh")
    shards_n = lax.axis_size(NARROW)
    r1 = w_first.shape[0] // halves
    r2 = w_second.shape[0] // halves
    mine = jnp.concatenate(
        [
            lax.dynamic_slice_in_dim(w_first, h * r1, r1, axis=0),
            lax.dynamic_slice_in_dim(w_second, h * r2, r2, axis=0),
        ],
        axis=0,
    )
    got = lax.all_gather(mine, ("zh",) + NARROW, axis=0, tiled=False)
    got = got.reshape(halves, shards_n, r1 + r2, got.shape[-1])
    return got[:, :, :r1], got[:, :, r1:]


def split_rows(x, like):
    halves, shards_n, r = like.shape[:3]
    return x.reshape(x.shape[0], shards_n, halves, r)


def shards(
    tile_pool,
    batch_index,
    pair_label,
    w_first,
    w_second,
    m_first,
    m_second,
    v_first,
    v_second,
    mom_first,
    mom_second,
):
    inputs = jnp.take(tile_pool[0], batch_index[0], axis=0)
    partner = pair_label[0]
    scale_one = 1.0 / math.sqrt(PIX)
    scale_two = 1.0 / math.sqrt(MID)
    first_whole, second_whole = gather_weights(w_first, w_second)
    hidden = (
        jnp.einsum("bnhr,hnrc->bc", split_rows(inputs, first_whole), first_whole,
                   preferred_element_type=jnp.float32)
        * scale_one
    )
    active_full, gelu_back = jax.vjp(jax.nn.gelu, hidden)
    active = active_full.astype(jnp.bfloat16)
    embedded = (
        jnp.einsum("bnhr,hnrc->bc", split_rows(active, second_whole), second_whole,
                   preferred_element_type=jnp.float32)
        * scale_two
    )
    embed_half = embed_gradient(embedded, partner)
    grad_second = lax.psum_scatter(
        (scale_two * jnp.dot(active.T, embed_half, preferred_element_type=jnp.float32)).astype(
            jnp.bfloat16
        ),
        NARROW,
        scatter_dimension=0,
        tiled=True,
    ).astype(jnp.float32)
    active_grad = scale_two * jnp.einsum(
        "bc,hnrc->bnhr", embed_half, second_whole, preferred_element_type=jnp.float32
    ).reshape(active.shape)
    hidden_half = gelu_back(active_grad)[0].astype(jnp.bfloat16)
    term_first = (
        scale_one * jnp.dot(inputs.T, hidden_half, preferred_element_type=jnp.float32)
    ).astype(jnp.bfloat16)
    term_first, grad_second = lax.optimization_barrier((term_first, grad_second))
    delta_second = adam_delta(grad_second, m_second[0], v_second[0], w_second)
    part_second = plane_sum(delta_second)
    grad_first = lax.psum_scatter(
        term_first, NARROW, scatter_dimension=0, tiled=True
    ).astype(jnp.float32)
    delta_first = adam_delta(grad_first, m_first[0], v_first[0], w_first)
    part_first = plane_sum(delta_first)
    rows_first = w_first.shape[0]
    new_w, vel = wide_mean_update(
        None,
        jnp.concatenate([mom_first, mom_second], axis=0),
        jnp.concatenate([w_first, w_second], axis=0),
        jnp.concatenate([part_first, part_second], axis=0),
    )
    return (new_w[:rows_first], new_w[rows_first:], vel[:rows_first], vel[rows_first:])


def solution(mesh):
    zh, y, x = 2, 4, 4
    devices = np.asarray(mesh.devices)
    wide, narrow = devices.shape
    sub = Mesh(devices.reshape(zh, y, x, narrow // 2, 2), WIDE + NARROW)
    site = P(WIDE, NARROW, None)
    rows = P(NARROW, None)
    return jax.shard_map(
        shards,
        mesh=sub,
        in_specs=(site, P(WIDE, NARROW), P(WIDE, NARROW), rows, rows, site, site, site, site, rows, rows),
        out_specs=(rows, rows, rows, rows),
        check_vma=False,
    )
```
